128 devices in a mesh: row: 8 (over z, y_hi), col: 16 (over y_lo, x, core).
Axes of the slice: x: 4, y: 4 (y_hi: 2, y_lo: 2; y = y_hi * 2 + y_lo), z: 4, core: 2. Of those that a mesh axis runs over, the one named last changes fastest.
Arguments:
- ancestor: float32 [16384, 16384], P('row', 'col'), may hold values from -6 to 6
- factor: float32 [2, 16384, 512], P(None, ('row', 'col')), may hold values from -0.0625 to 0.0625
- diag_inverse: float32 [2, 512, 512], replicated, may hold values from -6 to 6
- structure: int32 [2, 16], replicated, may hold values from 0 to 31, as said below
Outputs:
- off_diagonal: float32 [2, 16384, 512], P(None, ('row', 'col'))
- diag_block: float32 [2, 512, 512], replicated
The draws below stay inside these ranges and needn't reach their ends.
Inputs may be any that keep to these rules, and one draw needn't show every extreme that they name: `structure`: each row holds 16 distinct tile indices; tile t covers rows t * 512 to t * 512 + 511.
All inputs are finite; a program needn't handle non-finite values.
Results may differ from the reference program's by a relative error of at most 0.0001.
Values sent between devices are 32-bit elements; how exact they have to be, the bound alone decides.
No kernel may reach another device: no remote copies, remote signals or barrier semaphores. Data moves between devices by JAX's collectives and lax.ppermute only.
A program may use at most 128 MiB of HBM per device.

```python
import jax
import jax.numpy as jnp
from jax import lax

ORDER = 16384
TILE = 512
WIDTH = 512
LIST = 16


def draw_structure(key, part):
    chosen = []
    for supernode in range(2):
        shuffled = jax.random.permutation(jax.random.fold_in(key, 11 + supernode), ORDER // TILE)
        chosen.append(shuffled[:LIST])
    return jnp.stack(chosen).astype(jnp.int32)


def level_of(stream_key, dims, split, low, top_value):
    def one(position, blocks):
        draws = jax.random.uniform(jax.random.fold_in(jax.random.fold_in(stream_key, 6), position), (blocks,), jnp.float32, low / len(split), top_value / len(split))
        return jnp.repeat(jnp.exp(draws), dims[position] // blocks).reshape((-1,) + (1,) * (len(dims) - position - 1))

    level = one(*split[0])
    for cut in split[1:]:
        level = level * one(*cut)
    return level


def bell_draw(rng, shape, scale, reach, pieces=(), kind=jnp.bfloat16):
    entries = scale * jax.random.normal(rng, shape, jnp.float32)
    if pieces:
        entries = entries * level_of(rng, shape, pieces, -0.22, 0.18)
    return jnp.clip(entries, -reach, reach).astype(kind)


def setup_inputs(seed: int = 0) -> dict:
    streams_of = jax.random.split(jax.random.key(seed), 5)
    ancestor = bell_draw(streams_of[0], (ORDER, ORDER), 1.0, 6.0, ((0, 8), (1, 16)), jnp.float32)
    factor = bell_draw(streams_of[1], (2, ORDER, WIDTH), (LIST * TILE) ** -0.5, 0.0625, ((1, 128),), jnp.float32)
    diag_inverse = bell_draw(streams_of[2], (2, WIDTH, WIDTH), 1.0, 6.0, (), jnp.float32)
    structure = draw_structure(jax.random.fold_in(streams_of[4], 71), 0)
    return dict(ancestor=ancestor, factor=factor, diag_inverse=diag_inverse, structure=structure)


exact_mode = lax.Precision.HIGHEST


def reference(ancestor, factor, diag_inverse, structure):
    off_blocks = []
    diag_blocks = []
    for supernode in range(2):
        row_ids = (structure[supernode][:, None] * TILE + jnp.arange(TILE, dtype=jnp.int32)[None, :]).reshape(-1).astype(jnp.int32)
        sub_matrix = jnp.take(jnp.take(ancestor, row_ids, axis=0), row_ids, axis=1)
        sub_factor = jnp.take(factor[supernode], row_ids, axis=0)
        panel_rows = jnp.dot(sub_matrix, sub_factor, precision=exact_mode, preferred_element_type=jnp.float32)
        dense_rows = jnp.zeros((ORDER, WIDTH), jnp.float32).at[row_ids].set(panel_rows)
        off_blocks.append(-dense_rows)
        diag_blocks.append(diag_inverse[supernode] + jnp.dot(sub_factor.T, panel_rows, precision=exact_mode, preferred_element_type=jnp.float32))
    return jnp.stack(off_blocks), jnp.stack(diag_blocks)
```

```python
import jax
import jax.numpy as jnp
from jax import lax
from jax.experimental import pallas as pl
from jax.experimental.pallas import tpu as pltpu
from jax.sharding import PartitionSpec as P

TILE = 512
WIDTH = 512

AXES = ("row", "col")


def route(move):
    pairs = []
    for d in range(128):
        z, yh, yl, x, core = d // 32, d // 16 % 2, d // 8 % 2, d // 2 % 4, d % 2
        z, y, x, core = move(z, yh * 2 + yl, x, core)
        z, y, x = z % 4, y % 4, x % 4
        pairs.append((d, z * 32 + (y // 2) * 16 + (y % 2) * 8 + x * 2 + core))
    return pairs


def to_core(v):
    return lax.ppermute(v, AXES, route(lambda z, y, x, c: (z, y, x, 1 - c)))


def to_x(v, s):
    return lax.ppermute(v, AXES, route(lambda z, y, x, c: (z, y, x + s, c)))


def to_y(v, s):
    return lax.ppermute(v, AXES, route(lambda z, y, x, c: (z, y + s, x, c)))


def to_yl(v):
    return lax.ppermute(v, AXES, route(lambda z, y, x, c: (z, y ^ 1, x, c)))


def to_z(v, s):
    return lax.ppermute(v, AXES, route(lambda z, y, x, c: (z + s, y, x, c)))


def halves(a):
    hi = a.astype(jnp.bfloat16)
    return hi, (a - hi.astype(jnp.float32)).astype(jnp.bfloat16)


def panel_kernel(info, own, oth, f0, f1, f2, f3, g_own, g_oth, *rest):
    outs, (f_hi, f_lo, acc) = rest[:6], rest[6:]
    i, j = pl.program_id(0), pl.program_id(1)
    core, z, yh, x, yl = info[8], info[9], info[10], info[11], info[12]

    @pl.when((i == 0) & (j == 0))
    def _():
        def place(value, col, row):
            at = pl.ds(pl.multiple_of(col * 128 + row * 16, 16), 16)
            hi, lo = halves(value)
            f_hi[at, :] = hi
            f_lo[at, :] = lo

        for s, ref in enumerate((f0, f1, f2, f3)):
            from_z = lax.rem(z + 4 - s, 4)

            @pl.loop(0, 8)
            def _(col):
                for h in range(2):
                    place(ref[h, col], col, from_z * 2 + h)

        for ref, from_yh in ((g_own, yh), (g_oth, 1 - yh)):
            for s in range(4):
                from_z = lax.rem(z + 4 - s, 4)

                @pl.loop(0, 8)
                def _(col):
                    place(ref[s, col], col + 8, from_z * 2 + from_yh)

    @pl.when(j == 0)
    def _():
        acc[...] = jnp.zeros_like(acc)

    for ref, side in ((own, core), (oth, 1 - core)):
        tile = side * 2 + j

        @pl.when((info[i] > 0) & (info[4 + tile] > 0))
        def _():
            at = pl.ds(pl.multiple_of(tile * TILE, TILE), TILE)
            hi, lo = halves(ref[...])
            b_hi = f_hi[at, :]
            acc[...] += (
                jnp.dot(hi, b_hi, preferred_element_type=jnp.float32)
                + jnp.dot(lo, b_hi, preferred_element_type=jnp.float32)
                + jnp.dot(hi, f_lo[at, :], preferred_element_type=jnp.float32)
            )

    @pl.when(j == 1)
    def _():
        to_l = lax.div(i, 2)
        for b in range(2):
            step = lax.rem(lax.rem(i, 2) * 2 + b + 4 - x, 4)
            first = acc[b * 256 : b * 256 + 128, :]
            last = acc[b * 256 + 128 : b * 256 + 256, :]
            for s in range(4):

                @pl.when(step == s)
                def _():
                    outs[s][to_l] = first

            @pl.when(to_l == yl)
            def _():
                outs[4][step] = last

            @pl.when(to_l != yl)
            def _():
                outs[5][step] = last


def panel(info, own, oth, pieces):
    whole = lambda v: pl.BlockSpec(v.shape, lambda i, j, info: (0,) * v.ndim)
    block = pl.BlockSpec((TILE, TILE), lambda i, j, info: (i, j))
    out = [jax.ShapeDtypeStruct((2, 128, WIDTH), jnp.float32)] * 4
    out += [jax.ShapeDtypeStruct((4, 128, WIDTH), jnp.float32)] * 2
    return pl.pallas_call(
        panel_kernel,
        grid_spec=pltpu.PrefetchScalarGridSpec(
            num_scalar_prefetch=1,
            grid=(4, 2),
            in_specs=[block, block] + [whole(v) for v in pieces],
            out_specs=[whole(v) for v in out],
            scratch_shapes=[
                pltpu.VMEM((2048, WIDTH), jnp.bfloat16),
                pltpu.VMEM((2048, WIDTH), jnp.bfloat16),
                pltpu.VMEM((TILE, WIDTH), jnp.float32),
            ],
        ),
        out_shape=out,
        compiler_params=pltpu.CompilerParams(vmem_limit_bytes=48 << 20),
        cost_estimate=pl.CostEstimate(
            flops=3 * 2 * 2048 * 2048 * 512, bytes_accessed=24 << 20, transcendentals=0
        ),
    )(info, own, oth, *pieces)


def scatter_sum(v, move, place):
    part = v.shape[0] // 4
    cut = lambda s: lax.dynamic_slice_in_dim(v, (place + s) % 4 * part, part, 0)
    got = [move(cut(s), s) for s in (1, 3, 2)]
    return cut(0) + got[0] + got[1] + got[2]


def collect(v, move, place):
    part = v.shape[0]
    one, three, two = (move(v, s) for s in (1, 3, 2))
    rolled = jnp.concatenate([v, three, two, one] * 2)
    return lax.dynamic_slice_in_dim(rolled, (4 - place) % 4 * part, 4 * part, 0)


def per_device(ancestor, factor, diag_inverse, structure):
    row, col = lax.axis_index("row"), lax.axis_index("col")
    z, yh = row // 2, row % 2
    yl, x, core = col // 8, col // 2 % 4, col % 2
    y = yh * 2 + yl
    group = yl * 4 + x

    oth = to_core(ancestor)
    f_keep = lax.dynamic_index_in_dim(factor, core, 0, keepdims=False)
    f_got = to_core(lax.dynamic_index_in_dim(factor, 1 - core, 0, keepdims=False))

    spread = lax.all_to_all(factor.reshape(2, 8, 16, WIDTH), "row", 1, 0)
    spread = lax.all_to_all(spread.reshape(16, 16, WIDTH), "col", 0, 0)
    low, high = spread[:8], spread[8:]
    low_y = to_y(low, 2)
    high_z = [high] + [to_z(high, s) for s in (1, 2, 3)]
    pair = jnp.where(yh == 0, jnp.stack([low, low_y]), jnp.stack([low_y, low]))
    pairs = [pair] + [to_z(pair, s) for s in (1, 2, 3)]
    quad = jnp.stack(high_z)
    quad_y = to_y(quad, 2)

    listed = lax.dynamic_index_in_dim(structure, core, 0, keepdims=False)
    four = jnp.arange(4, dtype=jnp.int32)
    flag = lambda tiles: jnp.any(listed[None, :] == tiles[:, None], axis=1)
    info = jnp.concatenate(
        [
            flag(row * 4 + four).astype(jnp.int32),
            flag(group * 4 + four).astype(jnp.int32),
            jnp.stack([core, z, yh, x, yl]).astype(jnp.int32),
        ]
    )
    first0, first1, first2, first3, last_keep, last_send = panel(
        info, ancestor, oth, [*pairs, quad, quad_y]
    )

    last_got = to_yl(last_send)
    got = [to_x(first1, 1), to_x(first3, 3), to_x(first2, 2)]
    first = first0 + got[0] + got[1] + got[2]
    cut = lambda v, i: lax.dynamic_index_in_dim(v, i, 0, keepdims=False)
    first = cut(first, yl) + to_yl(cut(first, 1 - yl))
    last = last_keep + last_got
    last = last[0] + to_x(last[1], 1) + to_x(last[3], 3) + to_x(last[2], 2)

    at_first = core == 0
    mine = jnp.where(at_first, first, last)
    theirs = to_core(jnp.where(at_first, last, first))
    off = -jnp.where(at_first, jnp.stack([mine, theirs]), jnp.stack([theirs, mine]))

    f_rows = jnp.where(
        at_first, jnp.concatenate([f_keep, f_got]), jnp.concatenate([f_got, f_keep])
    )
    diag = lax.dot_general(
        f_rows,
        jnp.concatenate([first, last]),
        (((0,), (0,)), ((), ())),
        precision=lax.Precision.HIGH,
        preferred_element_type=jnp.float32,
    )
    diag = scatter_sum(diag, to_x, x)
    diag = scatter_sum(diag, to_y, y)
    diag = scatter_sum(diag, to_z, z)
    diag = collect(diag, to_z, z)
    diag = collect(diag, to_y, y)
    diag = collect(diag, to_x, x)
    diag_oth = to_core(diag)
    both = jnp.where(
        at_first, jnp.stack([diag, diag_oth]), jnp.stack([diag_oth, diag])
    )
    return off, diag_inverse + both


def solution(mesh):
    in_specs = (P("row", "col"), P(None, ("row", "col"), None), P(), P())
    out_specs = (P(None, ("row", "col"), None), P())
    return jax.shard_map(
        per_device, mesh=mesh, in_specs=in_specs, out_specs=out_specs, check_vma=False
    )
```

```python
import jax
import jax.numpy as jnp
from jax import lax
from jax.experimental import pallas as pl
from jax.experimental.pallas import tpu as pltpu
from jax.sharding import Mesh
from jax.sharding import PartitionSpec as P

TILE = 512
WIDTH = 512

ROW, COL = ("z", "yh"), ("yl", "x", "core")
AXES, CHIPS = ROW + COL, ROW + COL[:2]


def route(move):
    pairs = []
    for d in range(128):
        z, yh, yl, x, core = d // 32, d // 16 % 2, d // 8 % 2, d // 2 % 4, d % 2
        z, y, x, core = move(z, yh * 2 + yl, x, core)
        z, y, x = z % 4, y % 4, x % 4
        pairs.append((d, z * 32 + (y // 2) * 16 + (y % 2) * 8 + x * 2 + core))
    return pairs


def to_core(v):
    return lax.ppermute(v, AXES, route(lambda z, y, x, c: (z, y, x, 1 - c)))


def to_x(v, s):
    return lax.ppermute(v, AXES, route(lambda z, y, x, c: (z, y, x + s, c)))


def to_y(v, s):
    return lax.ppermute(v, AXES, route(lambda z, y, x, c: (z, y + s, x, c)))


def to_yl(v):
    return lax.ppermute(v, AXES, route(lambda z, y, x, c: (z, y ^ 1, x, c)))


def to_z(v, s):
    return lax.ppermute(v, AXES, route(lambda z, y, x, c: (z + s, y, x, c)))


def halves(a):
    hi = a.astype(jnp.bfloat16)
    return hi, (a - hi.astype(jnp.float32)).astype(jnp.bfloat16)


def panel_kernel(info, own, oth, f0, f1, f2, f3, g_own, g_oth, *rest):
    outs, (f_hi, f_lo, acc) = rest[:6], rest[6:]
    i, j = pl.program_id(0), pl.program_id(1)
    core, z, yh, x, yl = info[8], info[9], info[10], info[11], info[12]

    @pl.when((i == 0) & (j == 0))
    def _():
        def place(value, col, row):
            at = pl.ds(pl.multiple_of(col * 128 + row * 16, 16), 16)
            hi, lo = halves(value)
            f_hi[at, :] = hi
            f_lo[at, :] = lo

        for s, ref in enumerate((f0, f1, f2, f3)):
            from_z = lax.rem(z + 4 - s, 4)

            @pl.loop(0, 8)
            def _(col):
                for h in range(2):
                    place(ref[h, col], col, from_z * 2 + h)

        for ref, from_yh in ((g_own, yh), (g_oth, 1 - yh)):
            for s in range(4):
                from_z = lax.rem(z + 4 - s, 4)

                @pl.loop(0, 8)
                def _(col):
                    place(ref[s, col], col + 8, from_z * 2 + from_yh)

    @pl.when(j == 0)
    def _():
        acc[...] = jnp.zeros_like(acc)

    for ref, side in ((own, core), (oth, 1 - core)):
        tile = side * 2 + j

        @pl.when((info[i] > 0) & (info[4 + tile] > 0))
        def _():
            at = pl.ds(pl.multiple_of(tile * TILE, TILE), TILE)
            hi, lo = halves(ref[...])
            b_hi = f_hi[at, :]
            acc[...] += (
                jnp.dot(hi, b_hi, preferred_element_type=jnp.float32)
                + jnp.dot(lo, b_hi, preferred_element_type=jnp.float32)
                + jnp.dot(hi, f_lo[at, :], preferred_element_type=jnp.float32)
            )

    @pl.when(j == 1)
    def _():
        to_l = lax.div(i, 2)
        for b in range(2):
            step = lax.rem(lax.rem(i, 2) * 2 + b + 4 - x, 4)
            first = acc[b * 256 : b * 256 + 128, :]
            last = acc[b * 256 + 128 : b * 256 + 256, :]
            for s in range(4):

                @pl.when(step == s)
                def _():
                    outs[s][to_l] = first

            @pl.when(to_l == yl)
            def _():
                outs[4][step] = last

            @pl.when(to_l != yl)
            def _():
                outs[5][step] = last


def panel(info, own, oth, pieces):
    whole = lambda v: pl.BlockSpec(v.shape, lambda i, j, info: (0,) * v.ndim)
    block = pl.BlockSpec((TILE, TILE), lambda i, j, info: (i, j))
    out = [jax.ShapeDtypeStruct((2, 128, WIDTH), jnp.float32)] * 4
    out += [jax.ShapeDtypeStruct((4, 128, WIDTH), jnp.float32)] * 2
    return pl.pallas_call(
        panel_kernel,
        grid_spec=pltpu.PrefetchScalarGridSpec(
            num_scalar_prefetch=1,
            grid=(4, 2),
            in_specs=[block, block] + [whole(v) for v in pieces],
            out_specs=[whole(v) for v in out],
            scratch_shapes=[
                pltpu.VMEM((2048, WIDTH), jnp.bfloat16),
                pltpu.VMEM((2048, WIDTH), jnp.bfloat16),
                pltpu.VMEM((TILE, WIDTH), jnp.float32),
            ],
        ),
        out_shape=out,
        compiler_params=pltpu.CompilerParams(vmem_limit_bytes=48 << 20),
        cost_estimate=pl.CostEstimate(
            flops=3 * 2 * 2048 * 2048 * 512, bytes_accessed=24 << 20, transcendentals=0
        ),
    )(info, own, oth, *pieces)


def per_device(ancestor, factor, diag_inverse, structure):
    z, yh, yl, x, core = (lax.axis_index(axis) for axis in AXES)
    row, group = z * 2 + yh, yl * 4 + x

    f_keep = lax.dynamic_index_in_dim(factor, core, 0, keepdims=False)
    f_got = to_core(lax.dynamic_index_in_dim(factor, 1 - core, 0, keepdims=False))

    spread = lax.all_to_all(factor.reshape(2, 8, 16, WIDTH), ROW, 1, 0)
    spread = lax.all_to_all(spread.reshape(16, 16, WIDTH), COL, 0, 0)
    spread, ancestor = lax.optimization_barrier((spread, ancestor))
    oth = to_core(ancestor)
    low, high = spread[:8], spread[8:]
    low_y, *high_z = lax.optimization_barrier(
        (to_y(low, 2), high, *(to_z(high, s) for s in (1, 2, 3)))
    )
    pair = jnp.where(yh == 0, jnp.stack([low, low_y]), jnp.stack([low_y, low]))
    pairs = [pair] + [to_z(pair, s) for s in (1, 2, 3)]
    quad = jnp.stack(high_z)
    quad_y = to_y(quad, 2)

    listed = lax.dynamic_index_in_dim(structure, core, 0, keepdims=False)
    four = jnp.arange(4, dtype=jnp.int32)
    flag = lambda tiles: jnp.any(listed[None, :] == tiles[:, None], axis=1)
    info = jnp.concatenate(
        [
            flag(row * 4 + four).astype(jnp.int32),
            flag(group * 4 + four).astype(jnp.int32),
            jnp.stack([core, z, yh, x, yl]).astype(jnp.int32),
        ]
    )
    first0, first1, first2, first3, last_keep, last_send = panel(
        info, ancestor, oth, [*pairs, quad, quad_y]
    )

    last_got = to_yl(last_send)
    got = [to_x(first1, 1), to_x(first3, 3), to_x(first2, 2)]
    first = first0 + got[0] + got[1] + got[2]
    cut = lambda v, i: lax.dynamic_index_in_dim(v, i, 0, keepdims=False)
    first = cut(first, yl) + to_yl(cut(first, 1 - yl))
    last = last_keep + last_got
    last = last[0] + to_x(last[1], 1) + to_x(last[3], 3) + to_x(last[2], 2)

    at_first = core == 0
    mine = jnp.where(at_first, first, last)
    theirs = to_core(jnp.where(at_first, last, first))
    off = -jnp.where(at_first, jnp.stack([mine, theirs]), jnp.stack([theirs, mine]))

    f_rows = jnp.where(
        at_first, jnp.concatenate([f_keep, f_got]), jnp.concatenate([f_got, f_keep])
    )
    diag = lax.dot_general(
        f_rows,
        jnp.concatenate([first, last]),
        (((0,), (0,)), ((), ())),
        precision=lax.Precision.HIGH,
        preferred_element_type=jnp.float32,
    )
    diag = lax.all_to_all(diag.reshape(64, 8, WIDTH), CHIPS, 0, 0)
    diag = jnp.broadcast_to(jnp.sum(diag, axis=0), (64, 8, WIDTH))
    diag = lax.all_to_all(diag, CHIPS, 0, 0).reshape(WIDTH, WIDTH)
    diag_oth = to_core(diag)
    both = jnp.where(
        at_first, jnp.stack([diag, diag_oth]), jnp.stack([diag_oth, diag])
    )
    return off, diag_inverse + both


def solution(mesh):
    mesh = Mesh(mesh.devices.reshape(4, 2, 2, 4, 2), AXES)
    in_specs = (P(ROW, COL), P(None, AXES, None), P(), P())
    out_specs = (P(None, AXES, None), P())
    return jax.shard_map(
        per_device, mesh=mesh, in_specs=in_specs, out_specs=out_specs, check_vma=False
    )
```

```python
import jax
import jax.numpy as jnp
from jax import lax
from jax.experimental import pallas as pl
from jax.experimental.pallas import tpu as pltpu
from jax.sharding import Mesh
from jax.sharding import PartitionSpec as P

TILE = 512
WIDTH = 512

ROW, COL = ("z", "yh"), ("yl", "x", "core")
AXES, CHIPS = ROW + COL, ROW + COL[:2]


def route(move):
    pairs = []
    for d in range(128):
        z, yh, yl, x, core = d // 32, d // 16 % 2, d // 8 % 2, d // 2 % 4, d % 2
        z, y, x, core = move(z, yh * 2 + yl, x, core)
        z, y, x = z % 4, y % 4, x % 4
        pairs.append((d, z * 32 + (y // 2) * 16 + (y % 2) * 8 + x * 2 + core))
    return pairs


def to_core(v):
    return lax.ppermute(v, AXES, route(lambda z, y, x, c: (z, y, x, 1 - c)))


def to_x(v, s):
    return lax.ppermute(v, AXES, route(lambda z, y, x, c: (z, y, x + s, c)))


def to_y(v, s):
    return lax.ppermute(v, AXES, route(lambda z, y, x, c: (z, y + s, x, c)))


def to_yl(v):
    return lax.ppermute(v, AXES, route(lambda z, y, x, c: (z, y ^ 1, x, c)))


def to_z(v, s):
    return lax.ppermute(v, AXES, route(lambda z, y, x, c: (z + s, y, x, c)))


def halves(a):
    hi = a.astype(jnp.bfloat16)
    return hi, (a - hi.astype(jnp.float32)).astype(jnp.bfloat16)


def panel_kernel(info, own, oth, f0, f1, f2, f3, g_own, g_oth, *rest):
    outs, (f_hi, f_lo, acc) = rest[:6], rest[6:]
    i = pl.program_id(0)
    core, z, yh, x, yl = info[8], info[9], info[10], info[11], info[12]

    @pl.when(i == 0)
    def _():
        def place(value, col, row):
            at = pl.ds(pl.multiple_of(col * 128 + row * 16, 16), 16)
            hi, lo = halves(value)
            f_hi[at, :] = hi
            f_lo[at, :] = lo

        for s, ref in enumerate((f0, f1, f2, f3)):
            from_z = lax.rem(z + 4 - s, 4)

            @pl.loop(0, 8)
            def _(col):
                for h in range(2):
                    place(ref[h, col], col, from_z * 2 + h)

        for ref, from_yh in ((g_own, yh), (g_oth, 1 - yh)):
            for s in range(4):
                from_z = lax.rem(z + 4 - s, 4)

                @pl.loop(0, 8)
                def _(col):
                    place(ref[s, col], col + 8, from_z * 2 + from_yh)

    acc[...] = jnp.zeros_like(acc)
    for ref, side in ((own, core), (oth, 1 - core)):
        for j in range(2):
            tile = side * 2 + j

            @pl.when((info[i] > 0) & (info[4 + tile] > 0))
            def _():
                at = pl.ds(pl.multiple_of(tile * TILE, TILE), TILE)
                hi, lo = halves(ref[:, j * TILE : (j + 1) * TILE])
                b_hi = f_hi[at, :]
                acc[...] += (
                    jnp.dot(hi, b_hi, preferred_element_type=jnp.float32)
                    + jnp.dot(lo, b_hi, preferred_element_type=jnp.float32)
                    + jnp.dot(hi, f_lo[at, :], preferred_element_type=jnp.float32)
                )

    to_l = lax.div(i, 2)
    for b in range(2):
        step = lax.rem(lax.rem(i, 2) * 2 + b + 4 - x, 4)
        first = acc[b * 256 : b * 256 + 128, :]
        last = acc[b * 256 + 128 : b * 256 + 256, :]
        for s in range(4):

            @pl.when(step == s)
            def _():
                outs[s][to_l] = first

        @pl.when(to_l == yl)
        def _():
            outs[4][step] = last

        @pl.when(to_l != yl)
        def _():
            outs[5][step] = last


def panel(info, own, oth, pieces):
    cols = pieces[0].shape[-1]
    whole = lambda v: pl.BlockSpec(v.shape, lambda i, info: (0,) * len(v.shape))
    block = pl.BlockSpec((TILE, own.shape[1]), lambda i, info: (info[13 + i], 0))
    out = [jax.ShapeDtypeStruct((2, 128, cols), jnp.float32)] * 4
    out += [jax.ShapeDtypeStruct((4, 128, cols), jnp.float32)] * 2
    return pl.pallas_call(
        panel_kernel,
        grid_spec=pltpu.PrefetchScalarGridSpec(
            num_scalar_prefetch=1,
            grid=(4,),
            in_specs=[block, block] + [whole(v) for v in pieces],
            out_specs=[whole(v) for v in out],
            scratch_shapes=[
                pltpu.VMEM((2048, cols), jnp.bfloat16),
                pltpu.VMEM((2048, cols), jnp.bfloat16),
                pltpu.VMEM((TILE, cols), jnp.float32),
            ],
        ),
        out_shape=out,
        compiler_params=pltpu.CompilerParams(vmem_limit_bytes=44 << 20),
        cost_estimate=pl.CostEstimate(
            flops=3 * 2 * 2048 * 2048 * cols,
            bytes_accessed=20 << 20,
            transcendentals=0,
        ),
    )(info, own, oth, *pieces)


def product(left, right):
    return lax.dot_general(
        left,
        right,
        (((0,), (0,)), ((), ())),
        precision=lax.Precision.HIGH,
        preferred_element_type=jnp.float32,
    )


def pick(v, i):
    return lax.dynamic_index_in_dim(v, i, 0, keepdims=False)


def per_device(ancestor, factor, diag_inverse, structure):
    z, yh, yl, x, core = (lax.axis_index(axis) for axis in AXES)
    row, group = z * 2 + yh, yl * 4 + x
    at_first = core == 0
    half = WIDTH // 2

    f_keep = pick(factor, core)
    f_got = to_core(pick(factor, 1 - core))

    spread = lax.all_to_all(factor.reshape(2, 8, 16, WIDTH), ROW, 1, 0)
    spread = lax.all_to_all(spread.reshape(16, 16, WIDTH), COL, 0, 0)
    spread, ancestor, f_got = lax.optimization_barrier((spread, ancestor, f_got))
    oth = to_core(ancestor)
    low, high = spread[:8], spread[8:]
    low_y, *high_z = lax.optimization_barrier(
        (to_y(low, 2), high, *(to_z(high, s) for s in (1, 2, 3)))
    )
    f_first = jnp.where(at_first, f_keep, f_got)
    f_last = jnp.where(at_first, f_got, f_keep)
    pair = jnp.where(yh == 0, jnp.stack([low, low_y]), jnp.stack([low_y, low]))
    quad = jnp.stack(high_z)

    listed = pick(structure, core)
    four = jnp.arange(4, dtype=jnp.int32)
    flag = lambda tiles: jnp.any(listed[None, :] == tiles[:, None], axis=1)
    rows_on = flag(row * 4 + four)
    past = jnp.where(rows_on[None, :] & (four[None, :] <= four[:, None]), four[None, :], 0)
    info = jnp.concatenate(
        [
            rows_on.astype(jnp.int32),
            flag(group * 4 + four).astype(jnp.int32),
            jnp.stack([core, z, yh, x, yl]).astype(jnp.int32),
            jnp.max(past, axis=1),
        ]
    )

    gathered = []
    for c in range(2):
        cut = lambda v: v[..., c * half : (c + 1) * half]
        pairs = [cut(pair)] + [to_z(cut(pair), s) for s in (1, 2, 3)]
        gathered.append([*pairs, cut(quad), to_y(cut(quad), 2)])
    fy = to_yl(f_first)
    fx = [to_x(f_last, s) for s in (3, 2, 1)]
    f_firsts = jnp.where(yl == 0, jnp.stack([f_first, fy]), jnp.stack([fy, f_first]))
    f_lasts = jnp.stack([f_last, *fx])

    firsts, lasts, diags = [], [], []
    for c in range(2):
        first0, first1, first2, first3, last_keep, last_send = panel(
            info, ancestor, oth, gathered[c]
        )
        last_got = to_yl(last_send)
        got = [to_x(first1, 1), to_x(first3, 3), to_x(first2, 2)]
        first = first0 + got[0] + got[1] + got[2]
        last = last_keep + last_got
        firsts.append(first)
        lasts.append(last)
        diags.append(
            product(f_firsts.reshape(256, WIDTH), first.reshape(256, half))
            + product(f_lasts.reshape(512, WIDTH), last.reshape(512, half))
        )

    diag = jnp.concatenate(diags, axis=1)
    diag = lax.all_to_all(diag.reshape(64, 8, WIDTH), CHIPS, 0, 0)
    diag = jnp.sum(diag, axis=0)
    diag = jnp.broadcast_to(diag, (64, 8, WIDTH))
    diag = lax.all_to_all(diag, CHIPS, 0, 0).reshape(WIDTH, WIDTH)
    diag_oth = to_core(diag)
    both = jnp.where(
        at_first, jnp.stack([diag, diag_oth]), jnp.stack([diag_oth, diag])
    )

    first = jnp.stack(firsts, axis=1)
    last = jnp.stack(lasts, axis=1)
    first = pick(first, yl) + to_yl(pick(first, 1 - yl))
    last = last[0] + to_x(last[1], 1) + to_x(last[3], 3) + to_x(last[2], 2)
    mine = jnp.where(at_first, first, last)
    theirs = to_core(jnp.where(at_first, last, first))
    off = -jnp.where(at_first, jnp.stack([mine, theirs]), jnp.stack([theirs, mine]))
    off = jnp.concatenate([off[:, 0], off[:, 1]], axis=-1)
    return off, diag_inverse + both


def solution(mesh):
    mesh = Mesh(mesh.devices.reshape(4, 2, 2, 4, 2), AXES)
    in_specs = (P(ROW, COL), P(None, AXES, None), P(), P())
    out_specs = (P(None, AXES, None), P())

    return jax.shard_map(
        per_device, mesh=mesh, in_specs=in_specs, out_specs=out_specs, check_vma=False
    )
```

```python
import jax
import jax.numpy as jnp
from jax import lax
from jax.experimental import pallas as pl
from jax.experimental.pallas import tpu as pltpu
from jax.sharding import Mesh
from jax.sharding import PartitionSpec as P

TILE = 512
WIDTH = 512

ROW, COL = ("z", "yh"), ("yl", "x", "core")
AXES, CHIPS = ROW + COL, ROW + COL[:2]


def route(move):
    pairs = []
    for d in range(128):
        z, yh, yl, x, core = d // 32, d // 16 % 2, d // 8 % 2, d // 2 % 4, d % 2
        z, y, x, core = move(z, yh * 2 + yl, x, core)
        z, y, x = z % 4, y % 4, x % 4
        pairs.append((d, z * 32 + (y // 2) * 16 + (y % 2) * 8 + x * 2 + core))
    return pairs


def to_core(v):
    return lax.ppermute(v, AXES, route(lambda z, y, x, c: (z, y, x, 1 - c)))


def to_x(v, s):
    return lax.ppermute(v, AXES, route(lambda z, y, x, c: (z, y, x + s, c)))


def to_y(v, s):
    return lax.ppermute(v, AXES, route(lambda z, y, x, c: (z, y + s, x, c)))


def to_yl(v):
    return lax.ppermute(v, AXES, route(lambda z, y, x, c: (z, y ^ 1, x, c)))


def to_z(v, s):
    return lax.ppermute(v, AXES, route(lambda z, y, x, c: (z + s, y, x, c)))


def halves(a):
    hi = a.astype(jnp.bfloat16)
    return hi, (a - hi.astype(jnp.float32)).astype(jnp.bfloat16)


def prepare_kernel(a, hi, lo):
    def step(a, hi, lo):
        hi[...], lo[...] = halves(a[...])

    spec = pl.BlockSpec((256, a.shape[1]), lambda i: (i, 0))
    pltpu.emit_pipeline(
        step, grid=(a.shape[0] // 256,), in_specs=[spec], out_specs=[spec, spec]
    )(a, hi, lo)


def prepare(a):
    spec = pl.BlockSpec(memory_space=pltpu.HBM)
    out = jax.ShapeDtypeStruct(a.shape, jnp.bfloat16)
    return pl.pallas_call(
        prepare_kernel,
        in_specs=[spec],
        out_specs=[spec, spec],
        out_shape=[out, out],
        compiler_params=pltpu.CompilerParams(vmem_limit_bytes=54 << 20),
        cost_estimate=pl.CostEstimate(
            flops=4 * a.size, bytes_accessed=8 * a.size, transcendentals=0
        ),
    )(a)


def panel_kernel(info, own_hi, own_lo, oth_hi, oth_lo, *rest):
    (f0, f1, f2, f3, g_own, g_oth), outs, (f_hi, f_lo, acc) = rest[:6], rest[6:12], rest[12:]
    core, z, yh, x, yl = info[8], info[9], info[10], info[11], info[12]

    def place(value, col, row):
        at = pl.ds(pl.multiple_of(col * 128 + row * 16, 16), 16)
        hi, lo = halves(value)
        f_hi[at, :] = hi
        f_lo[at, :] = lo

    i = pl.program_id(0)

    @pl.when(i == 0)
    def _():
        for s, ref in enumerate((f0, f1, f2, f3)):
            from_z = lax.rem(z + 4 - s, 4)
            for h, from_yh in enumerate((yh, 1 - yh)):
                for col in range(8):
                    place(ref[h, col], col, from_z * 2 + from_yh)

        for ref, from_yh in ((g_own, yh), (g_oth, 1 - yh)):
            for s in range(4):
                from_z = lax.rem(z + 4 - s, 4)
                for col in range(8):
                    place(ref[s, col], col + 8, from_z * 2 + from_yh)

    acc[...] = jnp.zeros_like(acc)
    for a_hi, a_lo, side in ((own_hi, own_lo, core), (oth_hi, oth_lo, 1 - core)):
        for j in range(2):
            tile = side * 2 + j

            @pl.when((info[i] > 0) & (info[4 + tile] > 0))
            def _():
                at = pl.ds(pl.multiple_of(tile * TILE, TILE), TILE)
                cols = slice(j * TILE, (j + 1) * TILE)
                hi, b_hi = a_hi[:, cols], f_hi[at, :]
                acc[...] += (
                    jnp.dot(hi, b_hi, preferred_element_type=jnp.float32)
                    + jnp.dot(a_lo[:, cols], b_hi, preferred_element_type=jnp.float32)
                    + jnp.dot(hi, f_lo[at, :], preferred_element_type=jnp.float32)
                )

    to_l = lax.div(i, 2)
    for b in range(2):
        step = lax.rem(lax.rem(i, 2) * 2 + b + 4 - x, 4)
        first = acc[b * 256 : b * 256 + 128, :]
        last = acc[b * 256 + 128 : b * 256 + 256, :]
        for s in range(4):

            @pl.when(step == s)
            def _():
                outs[s][to_l] = first

        @pl.when(to_l == yl)
        def _():
            outs[4][step] = last

        @pl.when(to_l != yl)
        def _():
            outs[5][step] = last


def in_vmem(n):
    return [pl.BlockSpec(memory_space=pltpu.VMEM)] * n


def panel(info, sides, pieces):
    cols = pieces[0].shape[-1]
    whole = lambda v: pl.BlockSpec(v.shape, lambda i, info: (0,) * len(v.shape))
    block = pl.BlockSpec((TILE, sides[0].shape[1]), lambda i, info: (info[13 + i], 0))
    out = [jax.ShapeDtypeStruct((2, 128, cols), jnp.float32)] * 4
    out += [jax.ShapeDtypeStruct((4, 128, cols), jnp.float32)] * 2
    return pl.pallas_call(
        panel_kernel,
        grid_spec=pltpu.PrefetchScalarGridSpec(
            num_scalar_prefetch=1,
            grid=(4,),
            in_specs=[block] * 4 + [whole(v) for v in pieces],
            out_specs=[whole(v) for v in out],
            scratch_shapes=[
                pltpu.VMEM((2048, cols), jnp.bfloat16),
                pltpu.VMEM((2048, cols), jnp.bfloat16),
                pltpu.VMEM((TILE, cols), jnp.float32),
            ],
        ),
        out_shape=out,
        compiler_params=pltpu.CompilerParams(vmem_limit_bytes=48 << 20),
        cost_estimate=pl.CostEstimate(
            flops=3 * 2 * 2048 * 2048 * cols,
            bytes_accessed=20 << 20,
            transcendentals=0,
        ),
    )(info, *sides, *pieces)


def finish_kernel(info, *refs):
    parts, rows, (diag, keep, send, *lasts) = refs[:12], refs[12:18], refs[18:]
    yl = info[12]
    t_hi, t_lo = halves(jnp.concatenate([ref[...] for ref in rows], axis=1))
    for c in range(2):
        firsts, (mine, got) = parts[c * 6 : c * 6 + 4], parts[c * 6 + 4 : c * 6 + 6]
        here, away = (sum(ref[i] for ref in firsts) for i in (yl, 1 - yl))
        sums = [here, away] + [mine[s] + got[s] for s in range(4)]
        for ref, value in zip((keep, send, *lasts), sums):
            ref[c] = value
        p_hi, p_lo = halves(jnp.concatenate(sums, axis=0))
        cols = p_hi.shape[1]
        diag[:, c * cols : (c + 1) * cols] = (
            jnp.dot(t_hi, p_hi, preferred_element_type=jnp.float32)
            + jnp.dot(t_lo, p_hi, preferred_element_type=jnp.float32)
            + jnp.dot(t_hi, p_lo, preferred_element_type=jnp.float32)
        )


def finish(info, parts, rows):
    cols = parts[0].shape[-1]
    out = [jax.ShapeDtypeStruct((WIDTH, 2 * cols), jnp.float32)]
    out += [jax.ShapeDtypeStruct((2, 128, cols), jnp.float32)] * 6
    return pl.pallas_call(
        finish_kernel,
        in_specs=[pl.BlockSpec(memory_space=pltpu.SMEM)] + in_vmem(18),
        out_specs=in_vmem(7),
        out_shape=out,
        compiler_params=pltpu.CompilerParams(vmem_limit_bytes=24 << 20),
        cost_estimate=pl.CostEstimate(
            flops=3 * 4 * 768 * WIDTH * cols, bytes_accessed=9 << 20, transcendentals=0
        ),
    )(info, *parts, *rows)


def pick(v, i):
    return lax.dynamic_index_in_dim(v, i, 0, keepdims=False)


def per_device(ancestor, factor, diag_inverse, structure):
    z, yh, yl, x, core = (lax.axis_index(axis) for axis in AXES)
    row, group = z * 2 + yh, yl * 4 + x
    at_first = core == 0
    half = WIDTH // 2

    listed = pick(structure, core)
    four = jnp.arange(4, dtype=jnp.int32)
    flag = lambda tiles: jnp.any(listed[None, :] == tiles[:, None], axis=1)
    rows_on = flag(row * 4 + four)
    past = jnp.where(rows_on[None, :] & (four[None, :] <= four[:, None]), four[None, :], 0)
    info = jnp.concatenate(
        [
            rows_on.astype(jnp.int32),
            flag(group * 4 + four).astype(jnp.int32),
            jnp.stack([core, z, yh, x, yl]).astype(jnp.int32),
            jnp.max(past, axis=1),
        ]
    )

    oth = to_core(ancestor)
    sides = prepare(ancestor)
    sides = [*sides, *prepare(oth)]

    turned = jnp.swapaxes(factor, 1, 2)
    f_keep = pick(turned, core)
    f_got = to_core(pick(turned, 1 - core))
    f_first = jnp.where(at_first, f_keep, f_got)
    f_last = jnp.where(at_first, f_got, f_keep)
    f_rows = [f_first, to_yl(f_first), f_last, *(to_x(f_last, s) for s in (3, 2, 1))]

    spread = lax.all_to_all(factor.reshape(2, 8, 16, WIDTH), ROW, 1, 0)
    spread = lax.all_to_all(spread.reshape(16, 16, WIDTH), COL, 0, 0)
    low, high = spread[:8], spread[8:]
    low_y, *high_z = lax.optimization_barrier(
        (to_y(low, 2), high, *(to_z(high, s) for s in (1, 2, 3)))
    )
    pair = jnp.stack([low, low_y])
    quad = jnp.stack(high_z)

    gathered = []
    for c in range(2):
        cut = lambda v: v[..., c * half : (c + 1) * half]
        pairs = [cut(pair)] + [to_z(cut(pair), s) for s in (1, 2, 3)]
        gathered.append([*pairs, cut(quad), to_y(cut(quad), 2)])

    parts = []
    for c in range(2):
        first0, first1, first2, first3, last_keep, last_send = panel(
            info, sides, gathered[c]
        )
        got = [to_x(first1, 1), to_x(first3, 3), to_x(first2, 2)]
        parts += [first0, *got, last_keep, to_yl(last_send)]

    diag, first, first_send, *last = finish(info, parts, f_rows)
    first = first + to_yl(first_send)
    last = last[0] + to_x(last[1], 1) + to_x(last[3], 3) + to_x(last[2], 2)
    mine = jnp.where(at_first, first, last)
    theirs = to_core(jnp.where(at_first, last, first))
    off = -jnp.where(at_first, jnp.stack([mine, theirs]), jnp.stack([theirs, mine]))
    off = jnp.concatenate([off[:, 0], off[:, 1]], axis=-1)

    diag = lax.all_to_all(diag.reshape(64, 8, WIDTH), CHIPS, 0, 0)
    own8 = ((row * 2 + yl) * 4 + x) * 8
    diag = jnp.sum(diag, axis=0)
    diag = diag + lax.dynamic_slice(diag_inverse, (core, own8, 0), (1, 8, WIDTH))[0]
    diag = lax.all_to_all(jnp.broadcast_to(diag, (64, 8, WIDTH)), CHIPS, 0, 0)
    diag = diag.reshape(WIDTH, WIDTH)
    diag_oth = to_core(diag)
    both = jnp.where(
        at_first, jnp.stack([diag, diag_oth]), jnp.stack([diag_oth, diag])
    )
    return off, both


def solution(mesh):
    mesh = Mesh(mesh.devices.reshape(4, 2, 2, 4, 2), AXES)
    in_specs = (P(ROW, COL), P(None, AXES, None), P(), P())
    out_specs = (P(None, AXES, None), P())

    return jax.shard_map(
        per_device, mesh=mesh, in_specs=in_specs, out_specs=out_specs, check_vma=False
    )
```

```python
import jax
import jax.numpy as jnp
from jax import lax
from jax.experimental import pallas as pl
from jax.experimental.pallas import tpu as pltpu
from jax.sharding import Mesh
from jax.sharding import PartitionSpec as P

TILE = 512
WIDTH = 512

ROW, COL = ("z", "yh"), ("yl", "x", "core")
AXES, CHIPS = ROW + COL, ROW + COL[:2]


def route(move):
    pairs = []
    for d in range(128):
        z, yh, yl, x, core = d // 32, d // 16 % 2, d // 8 % 2, d // 2 % 4, d % 2
        z, y, x, core = move(z, yh * 2 + yl, x, core)
        z, y, x = z % 4, y % 4, x % 4
        pairs.append((d, z * 32 + (y // 2) * 16 + (y % 2) * 8 + x * 2 + core))
    return pairs


def to_core(v):
    return lax.ppermute(v, AXES, route(lambda z, y, x, c: (z, y, x, 1 - c)))


def to_x(v, s):
    return lax.ppermute(v, AXES, route(lambda z, y, x, c: (z, y, x + s, c)))


def to_y(v, s):
    return lax.ppermute(v, AXES, route(lambda z, y, x, c: (z, y + s, x, c)))


def to_yl(v):
    return lax.ppermute(v, AXES, route(lambda z, y, x, c: (z, y ^ 1, x, c)))


def to_z(v, s):
    return lax.ppermute(v, AXES, route(lambda z, y, x, c: (z + s, y, x, c)))


def halves(a):
    hi = a.astype(jnp.bfloat16)
    return hi, (a - hi.astype(jnp.float32)).astype(jnp.bfloat16)


def panel_kernel(info, own, oth, *rest):
    (f0, f1, f2, f3, g_own, g_oth), outs, (f_hi, f_lo, acc) = rest[:6], rest[6:12], rest[12:]
    core, z, yh, x, yl = info[8], info[9], info[10], info[11], info[12]

    def place(value, col, row):
        at = pl.ds(pl.multiple_of(col * 128 + row * 16, 16), 16)
        hi, lo = halves(value)
        f_hi[at, :] = hi
        f_lo[at, :] = lo

    i = pl.program_id(0)

    @pl.when(i == 0)
    def _():
        for s, ref in enumerate((f0, f1, f2, f3)):
            from_z = lax.rem(z + 4 - s, 4)
            for h, from_yh in enumerate((yh, 1 - yh)):
                for col in range(8):
                    place(ref[h, col], col, from_z * 2 + from_yh)

        for ref, from_yh in ((g_own, yh), (g_oth, 1 - yh)):
            for s in range(4):
                from_z = lax.rem(z + 4 - s, 4)
                for col in range(8):
                    place(ref[s, col], col + 8, from_z * 2 + from_yh)

    acc[...] = jnp.zeros_like(acc)
    for ref, side in ((own, core), (oth, 1 - core)):
        for j in range(2):
            tile = side * 2 + j

            @pl.when((info[i] > 0) & (info[4 + tile] > 0))
            def _():
                at = pl.ds(pl.multiple_of(tile * TILE, TILE), TILE)
                hi, lo = halves(ref[:, j * TILE : (j + 1) * TILE])
                b_hi = f_hi[at, :]
                acc[...] += (
                    jnp.dot(hi, b_hi, preferred_element_type=jnp.float32)
                    + jnp.dot(lo, b_hi, preferred_element_type=jnp.float32)
                    + jnp.dot(hi, f_lo[at, :], preferred_element_type=jnp.float32)
                )

    to_l = lax.div(i, 2)
    for b in range(2):
        step = lax.rem(lax.rem(i, 2) * 2 + b + 4 - x, 4)
        first = acc[b * 256 : b * 256 + 128, :]
        last = acc[b * 256 + 128 : b * 256 + 256, :]
        for s in range(4):

            @pl.when(step == s)
            def _():
                outs[s][to_l] = first

        @pl.when(to_l == yl)
        def _():
            outs[4][step] = last

        @pl.when(to_l != yl)
        def _():
            outs[5][step] = last


def in_vmem(n):
    return [pl.BlockSpec(memory_space=pltpu.VMEM)] * n


def panel(info, own, oth, pieces):
    cols = pieces[0].shape[-1]
    whole = lambda v: pl.BlockSpec(v.shape, lambda i, info: (0,) * len(v.shape))
    block = pl.BlockSpec((TILE, own.shape[1]), lambda i, info: (info[13 + i], 0))
    out = [jax.ShapeDtypeStruct((2, 128, cols), jnp.float32)] * 4
    out += [jax.ShapeDtypeStruct((4, 128, cols), jnp.float32)] * 2
    return pl.pallas_call(
        panel_kernel,
        grid_spec=pltpu.PrefetchScalarGridSpec(
            num_scalar_prefetch=1,
            grid=(4,),
            in_specs=[block] * 2 + [whole(v) for v in pieces],
            out_specs=[whole(v) for v in out],
            scratch_shapes=[
                pltpu.VMEM((2048, cols), jnp.bfloat16),
                pltpu.VMEM((2048, cols), jnp.bfloat16),
                pltpu.VMEM((TILE, cols), jnp.float32),
            ],
        ),
        out_shape=out,
        compiler_params=pltpu.CompilerParams(vmem_limit_bytes=48 << 20),
        cost_estimate=pl.CostEstimate(
            flops=3 * 2 * 2048 * 2048 * cols,
            bytes_accessed=20 << 20,
            transcendentals=0,
        ),
    )(info, own, oth, *pieces)


def finish_kernel(info, *refs):
    parts, rows, (diag, keep, send, *lasts) = refs[:12], refs[12:18], refs[18:]
    yl = info[12]
    t_hi, t_lo = halves(jnp.concatenate([ref[...] for ref in rows], axis=1))
    for c in range(2):
        firsts, (mine, got) = parts[c * 6 : c * 6 + 4], parts[c * 6 + 4 : c * 6 + 6]
        here, away = (sum(ref[i] for ref in firsts) for i in (yl, 1 - yl))
        sums = [here, away] + [mine[s] + got[s] for s in range(4)]
        for ref, value in zip((keep, send, *lasts), sums):
            ref[c] = value
        p_hi, p_lo = halves(jnp.concatenate(sums, axis=0))
        cols = p_hi.shape[1]
        diag[:, c * cols : (c + 1) * cols] = (
            jnp.dot(t_hi, p_hi, preferred_element_type=jnp.float32)
            + jnp.dot(t_lo, p_hi, preferred_element_type=jnp.float32)
            + jnp.dot(t_hi, p_lo, preferred_element_type=jnp.float32)
        )


def finish(info, parts, rows):
    cols = parts[0].shape[-1]
    out = [jax.ShapeDtypeStruct((WIDTH, 2 * cols), jnp.float32)]
    out += [jax.ShapeDtypeStruct((2, 128, cols), jnp.float32)] * 6
    return pl.pallas_call(
        finish_kernel,
        in_specs=[pl.BlockSpec(memory_space=pltpu.SMEM)] + in_vmem(18),
        out_specs=in_vmem(7),
        out_shape=out,
        compiler_params=pltpu.CompilerParams(vmem_limit_bytes=24 << 20),
        cost_estimate=pl.CostEstimate(
            flops=3 * 4 * 768 * WIDTH * cols, bytes_accessed=9 << 20, transcendentals=0
        ),
    )(info, *parts, *rows)


def pick(v, i):
    return lax.dynamic_index_in_dim(v, i, 0, keepdims=False)


def per_device(ancestor, factor, diag_inverse, structure):
    z, yh, yl, x, core = (lax.axis_index(axis) for axis in AXES)
    row, group = z * 2 + yh, yl * 4 + x
    at_first = core == 0
    half = WIDTH // 2

    listed = pick(structure, core)
    four = jnp.arange(4, dtype=jnp.int32)
    flag = lambda tiles: jnp.any(listed[None, :] == tiles[:, None], axis=1)
    rows_on = flag(row * 4 + four)
    past = jnp.where(rows_on[None, :] & (four[None, :] <= four[:, None]), four[None, :], 0)
    info = jnp.concatenate(
        [
            rows_on.astype(jnp.int32),
            flag(group * 4 + four).astype(jnp.int32),
            jnp.stack([core, z, yh, x, yl]).astype(jnp.int32),
            jnp.max(past, axis=1),
        ]
    )

    oth = to_core(ancestor)

    turned = jnp.swapaxes(factor, 1, 2)
    f_keep = pick(turned, core)
    f_got = to_core(pick(turned, 1 - core))
    f_first = jnp.where(at_first, f_keep, f_got)
    f_last = jnp.where(at_first, f_got, f_keep)
    f_rows = [f_first, to_yl(f_first), f_last, *(to_x(f_last, s) for s in (3, 2, 1))]

    spread = lax.all_to_all(factor.reshape(2, 8, 16, WIDTH), ROW, 1, 0)
    spread = lax.all_to_all(spread.reshape(16, 16, WIDTH), COL, 0, 0)
    low, high = spread[:8], spread[8:]
    low_y, *high_z = lax.optimization_barrier(
        (to_y(low, 2), high, *(to_z(high, s) for s in (1, 2, 3)))
    )
    pair = jnp.stack([low, low_y])
    quad = jnp.stack(high_z)

    gathered = []
    for c in range(2):
        cut = lambda v: v[..., c * half : (c + 1) * half]
        pairs = [cut(pair)] + [to_z(cut(pair), s) for s in (1, 2, 3)]
        gathered.append([*pairs, cut(quad), to_y(cut(quad), 2)])

    parts = []
    for c in range(2):
        first0, first1, first2, first3, last_keep, last_send = panel(
            info, ancestor, oth, gathered[c]
        )
        got = [to_x(first1, 1), to_x(first3, 3), to_x(first2, 2)]
        parts += [first0, *got, last_keep, to_yl(last_send)]

    diag, first, first_send, *last = finish(info, parts, f_rows)
    first = first + to_yl(first_send)
    last = last[0] + to_x(last[1], 1) + to_x(last[3], 3) + to_x(last[2], 2)
    mine = jnp.where(at_first, first, last)
    theirs = to_core(jnp.where(at_first, last, first))
    off = -jnp.where(at_first, jnp.stack([mine, theirs]), jnp.stack([theirs, mine]))
    off = jnp.concatenate([off[:, 0], off[:, 1]], axis=-1)

    diag = lax.all_to_all(diag.reshape(64, 8, WIDTH), CHIPS, 0, 0)
    own8 = ((row * 2 + yl) * 4 + x) * 8
    diag = jnp.sum(diag, axis=0)
    diag = diag + lax.dynamic_slice(diag_inverse, (core, own8, 0), (1, 8, WIDTH))[0]
    diag = lax.all_to_all(jnp.broadcast_to(diag, (64, 8, WIDTH)), CHIPS, 0, 0)
    diag = diag.reshape(WIDTH, WIDTH)
    diag_oth = to_core(diag)
    both = jnp.where(
        at_first, jnp.stack([diag, diag_oth]), jnp.stack([diag_oth, diag])
    )
    return off, both


def solution(mesh):
    mesh = Mesh(mesh.devices.reshape(4, 2, 2, 4, 2), AXES)
    in_specs = (P(ROW, COL), P(None, AXES, None), P(), P())
    out_specs = (P(None, AXES, None), P())

    return jax.shard_map(
        per_device, mesh=mesh, in_specs=in_specs, out_specs=out_specs, check_vma=False
    )
```

```python
import jax
import jax.numpy as jnp
from jax import lax
from jax.experimental import pallas as pl
from jax.experimental.pallas import tpu as pltpu
from jax.sharding import Mesh
from jax.sharding import PartitionSpec as P

TILE = 512
WIDTH = 512

ROW, COL = ("z", "yh"), ("yl", "x", "core")
AXES, CHIPS = ROW + COL, ROW + COL[:2]


def route(move):
    pairs = []
    for d in range(128):
        z, yh, yl, x, core = d // 32, d // 16 % 2, d // 8 % 2, d // 2 % 4, d % 2
        z, y, x, core = move(z, yh * 2 + yl, x, core)
        z, y, x = z % 4, y % 4, x % 4
        pairs.append((d, z * 32 + (y // 2) * 16 + (y % 2) * 8 + x * 2 + core))
    return pairs


def to_core(v):
    return lax.ppermute(v, AXES, route(lambda z, y, x, c: (z, y, x, 1 - c)))


def to_x(v, s):
    return lax.ppermute(v, AXES, route(lambda z, y, x, c: (z, y, x + s, c)))


def to_y(v, s):
    return lax.ppermute(v, AXES, route(lambda z, y, x, c: (z, y + s, x, c)))


def to_yl(v):
    return lax.ppermute(v, AXES, route(lambda z, y, x, c: (z, y ^ 1, x, c)))


def to_z(v, s):
    return lax.ppermute(v, AXES, route(lambda z, y, x, c: (z + s, y, x, c)))


def halves(a):
    hi = a.astype(jnp.bfloat16)
    return hi, (a - hi.astype(jnp.float32)).astype(jnp.bfloat16)


def panel_kernel(info, own, oth, *rest):
    (f0, f1, f2, f3, g_own, g_oth), outs, (f_hi, f_lo, acc) = rest[:6], rest[6:12], rest[12:]
    core, z, yh, x, yl = info[8], info[9], info[10], info[11], info[12]

    def place(value, col, row):
        at = pl.ds(pl.multiple_of(col * 128 + row * 16, 16), 16)
        hi, lo = halves(value)
        f_hi[at, :] = hi
        f_lo[at, :] = lo

    i = pl.program_id(0)

    @pl.when(i == 0)
    def _():
        for s, ref in enumerate((f0, f1, f2, f3)):
            from_z = lax.rem(z + 4 - s, 4)
            for h, from_yh in enumerate((yh, 1 - yh)):
                for col in range(8):
                    place(ref[h, col], col, from_z * 2 + from_yh)

        for ref, from_yh in ((g_own, yh), (g_oth, 1 - yh)):
            for s in range(4):
                from_z = lax.rem(z + 4 - s, 4)
                for col in range(8):
                    place(ref[s, col], col + 8, from_z * 2 + from_yh)

    acc[...] = jnp.zeros_like(acc)
    for ref, side in ((own, core), (oth, 1 - core)):
        for j in range(2):
            tile = side * 2 + j

            @pl.when((info[i] > 0) & (info[4 + tile] > 0))
            def _():
                at = pl.ds(pl.multiple_of(tile * TILE, TILE), TILE)
                hi, lo = halves(ref[:, j * TILE : (j + 1) * TILE])
                b_hi = f_hi[at, :]
                acc[...] += (
                    jnp.dot(hi, b_hi, preferred_element_type=jnp.float32)
                    + jnp.dot(lo, b_hi, preferred_element_type=jnp.float32)
                    + jnp.dot(hi, f_lo[at, :], preferred_element_type=jnp.float32)
                )

    to_l = lax.div(i, 2)
    for b in range(2):
        step = lax.rem(lax.rem(i, 2) * 2 + b + 4 - x, 4)
        first = acc[b * 256 : b * 256 + 128, :]
        last = acc[b * 256 + 128 : b * 256 + 256, :]
        for s in range(4):

            @pl.when(step == s)
            def _():
                outs[s][to_l] = first

        @pl.when(to_l == yl)
        def _():
            outs[4][step] = last

        @pl.when(to_l != yl)
        def _():
            outs[5][step] = last


def in_vmem(n):
    return [pl.BlockSpec(memory_space=pltpu.VMEM)] * n


def panel(info, own, oth, pieces):
    cols = pieces[0].shape[-1]
    whole = lambda v: pl.BlockSpec(v.shape, lambda i, info: (0,) * len(v.shape))
    block = pl.BlockSpec((TILE, own.shape[1]), lambda i, info: (info[13 + i], 0))
    out = [jax.ShapeDtypeStruct((2, 128, cols), jnp.float32)] * 4
    out += [jax.ShapeDtypeStruct((4, 128, cols), jnp.float32)] * 2
    return pl.pallas_call(
        panel_kernel,
        grid_spec=pltpu.PrefetchScalarGridSpec(
            num_scalar_prefetch=1,
            grid=(4,),
            in_specs=[block] * 2 + [whole(v) for v in pieces],
            out_specs=[whole(v) for v in out],
            scratch_shapes=[
                pltpu.VMEM((2048, cols), jnp.bfloat16),
                pltpu.VMEM((2048, cols), jnp.bfloat16),
                pltpu.VMEM((TILE, cols), jnp.float32),
            ],
        ),
        out_shape=out,
        compiler_params=pltpu.CompilerParams(vmem_limit_bytes=48 << 20),
        cost_estimate=pl.CostEstimate(
            flops=3 * 2 * 2048 * 2048 * cols,
            bytes_accessed=20 << 20,
            transcendentals=0,
        ),
    )(info, own, oth, *pieces)


def finish_kernel(info, *refs):
    parts, rows, (diag, keep, send, *lasts) = refs[:12], refs[12:18], refs[18:]
    yl = info[12]
    t_hi, t_lo = halves(jnp.concatenate([ref[...] for ref in rows], axis=1))
    for c in range(2):
        firsts, (mine, got) = parts[c * 6 : c * 6 + 4], parts[c * 6 + 4 : c * 6 + 6]
        here, away = (sum(ref[i] for ref in firsts) for i in (yl, 1 - yl))
        sums = [here, away] + [mine[s] + got[s] for s in range(4)]
        for ref, value in zip((keep, send, *lasts), sums):
            ref[c] = value
        p_hi, p_lo = halves(jnp.concatenate(sums, axis=0))
        cols = p_hi.shape[1]
        diag[:, c * cols : (c + 1) * cols] = (
            jnp.dot(t_hi, p_hi, preferred_element_type=jnp.float32)
            + jnp.dot(t_lo, p_hi, preferred_element_type=jnp.float32)
            + jnp.dot(t_hi, p_lo, preferred_element_type=jnp.float32)
        )


def finish(info, parts, rows):
    cols = parts[0].shape[-1]
    out = [jax.ShapeDtypeStruct((WIDTH, 2 * cols), jnp.float32)]
    out += [jax.ShapeDtypeStruct((2, 128, cols), jnp.float32)] * 6
    return pl.pallas_call(
        finish_kernel,
        in_specs=[pl.BlockSpec(memory_space=pltpu.SMEM)] + in_vmem(18),
        out_specs=in_vmem(7),
        out_shape=out,
        compiler_params=pltpu.CompilerParams(vmem_limit_bytes=24 << 20),
        cost_estimate=pl.CostEstimate(
            flops=3 * 4 * 768 * WIDTH * cols, bytes_accessed=9 << 20, transcendentals=0
        ),
    )(info, *parts, *rows)


def pick(v, i):
    return lax.dynamic_index_in_dim(v, i, 0, keepdims=False)


def per_device(ancestor, factor, diag_inverse, structure):
    z, yh, yl, x, core = (lax.axis_index(axis) for axis in AXES)
    row, group = z * 2 + yh, yl * 4 + x
    at_first = core == 0
    half = WIDTH // 2

    listed = pick(structure, core)
    four = jnp.arange(4, dtype=jnp.int32)
    flag = lambda tiles: jnp.any(listed[None, :] == tiles[:, None], axis=1)
    rows_on = flag(row * 4 + four)
    past = jnp.where(rows_on[None, :] & (four[None, :] <= four[:, None]), four[None, :], 0)
    info = jnp.concatenate(
        [
            rows_on.astype(jnp.int32),
            flag(group * 4 + four).astype(jnp.int32),
            jnp.stack([core, z, yh, x, yl]).astype(jnp.int32),
            jnp.max(past, axis=1),
        ]
    )

    oth = to_core(ancestor)

    turned = jnp.swapaxes(factor, 1, 2)
    f_keep = pick(turned, core)
    f_got = to_core(pick(turned, 1 - core))
    f_first = jnp.where(at_first, f_keep, f_got)
    f_last = jnp.where(at_first, f_got, f_keep)
    f_rows = [f_first, to_yl(f_first), f_last, *(to_x(f_last, s) for s in (3, 2, 1))]

    spread = lax.all_to_all(factor.reshape(2, 8, 16, WIDTH), ROW, 1, 0)
    spread = lax.all_to_all(spread.reshape(16, 16, WIDTH), COL, 0, 0)
    gathered = []
    for c in range(2):
        low, high = (v[:, :, c * half : (c + 1) * half] for v in (spread[:8], spread[8:]))
        low_y, *high_z = lax.optimization_barrier(
            (to_y(low, 2), high, *(to_z(high, s) for s in (1, 2, 3)))
        )
        pair, quad = jnp.stack([low, low_y]), jnp.stack(high_z)
        pairs = [pair] + [to_z(pair, s) for s in (1, 2, 3)]
        gathered.append([*pairs, quad, to_y(quad, 2)])

    parts = []
    for c in range(2):
        first0, first1, first2, first3, last_keep, last_send = panel(
            info, ancestor, oth, gathered[c]
        )
        got = [to_x(first1, 1), to_x(first3, 3), to_x(first2, 2)]
        parts += [first0, *got, last_keep, to_yl(last_send)]

    diag, first, first_send, *last = finish(info, parts, f_rows)
    first = first + to_yl(first_send)
    last = last[0] + to_x(last[1], 1) + to_x(last[3], 3) + to_x(last[2], 2)
    mine = jnp.where(at_first, first, last)
    theirs = to_core(jnp.where(at_first, last, first))
    off = -jnp.where(at_first, jnp.stack([mine, theirs]), jnp.stack([theirs, mine]))
    off = jnp.concatenate([off[:, 0], off[:, 1]], axis=-1)

    diag = lax.all_to_all(diag.reshape(64, 8, WIDTH), CHIPS, 0, 0)
    own8 = ((row * 2 + yl) * 4 + x) * 8
    diag = jnp.sum(diag, axis=0)
    diag = diag + lax.dynamic_slice(diag_inverse, (core, own8, 0), (1, 8, WIDTH))[0]
    diag = lax.all_to_all(jnp.broadcast_to(diag, (64, 8, WIDTH)), CHIPS, 0, 0)
    diag = diag.reshape(WIDTH, WIDTH)
    diag_oth = to_core(diag)
    both = jnp.where(
        at_first, jnp.stack([diag, diag_oth]), jnp.stack([diag_oth, diag])
    )
    return off, both


def solution(mesh):
    mesh = Mesh(mesh.devices.reshape(4, 2, 2, 4, 2), AXES)
    in_specs = (P(ROW, COL), P(None, AXES, None), P(), P())
    out_specs = (P(None, AXES, None), P())

    return jax.shard_map(
        per_device, mesh=mesh, in_specs=in_specs, out_specs=out_specs, check_vma=False
    )
```

```python
import jax
import jax.numpy as jnp
from jax import lax
from jax.experimental import pallas as pl
from jax.experimental.pallas import tpu as pltpu
from jax.sharding import Mesh
from jax.sharding import PartitionSpec as P

TILE = 512
WIDTH = 512

ROW, COL = ("z", "yh"), ("yl", "x", "core")
AXES, CHIPS = ROW + COL, ROW + COL[:2]


def route(move):
    pairs = []
    for d in range(128):
        z, yh, yl, x, core = d // 32, d // 16 % 2, d // 8 % 2, d // 2 % 4, d % 2
        z, y, x, core = move(z, yh * 2 + yl, x, core)
        z, y, x = z % 4, y % 4, x % 4
        pairs.append((d, z * 32 + (y // 2) * 16 + (y % 2) * 8 + x * 2 + core))
    return pairs


def to_core(v):
    return lax.ppermute(v, AXES, route(lambda z, y, x, c: (z, y, x, 1 - c)))


def to_x(v, s):
    return lax.ppermute(v, AXES, route(lambda z, y, x, c: (z, y, x + s, c)))


def to_y(v, s):
    return lax.ppermute(v, AXES, route(lambda z, y, x, c: (z, y + s, x, c)))


def to_yl(v):
    return lax.ppermute(v, AXES, route(lambda z, y, x, c: (z, y ^ 1, x, c)))


def to_z(v, s):
    return lax.ppermute(v, AXES, route(lambda z, y, x, c: (z + s, y, x, c)))


def halves(a):
    hi = a.astype(jnp.bfloat16)
    return hi, (a - hi.astype(jnp.float32)).astype(jnp.bfloat16)


def panel_kernel(info, own, oth, f0, f1, f2, f3, g_own, g_oth, *rest):
    outs, (f_hi, f_lo, acc, tiles, sems) = rest[:6], rest[6:]
    core, z, yh, x, yl = info[8], info[9], info[10], info[11], info[12]

    def each(i, act):
        rows = pl.ds(pl.multiple_of(i * TILE, TILE), TILE)
        for s, (ref, side) in enumerate(((own, core), (oth, 1 - core))):
            for j in range(2):
                slot, tile = s * 2 + j, side * 2 + j
                copy = pltpu.make_async_copy(
                    ref.at[rows, pl.ds(j * TILE, TILE)], tiles.at[i, slot], sems.at[i, slot]
                )

                @pl.when((info[i] > 0) & (info[4 + tile] > 0))
                def _():
                    act(copy, slot, tile)

    @pl.loop(0, 4)
    def _(i):
        each(i, lambda copy, slot, tile: copy.start())

    def place(value, col, row):
        at = pl.ds(pl.multiple_of(col * 128 + row * 16, 16), 16)
        hi, lo = halves(value)
        f_hi[at, :] = hi
        f_lo[at, :] = lo

    for s, ref in enumerate((f0, f1, f2, f3)):
        from_z = lax.rem(z + 4 - s, 4)
        for h, from_yh in enumerate((yh, 1 - yh)):
            for col in range(8):
                place(ref[h, col], col, from_z * 2 + from_yh)

    for ref, from_yh in ((g_own, yh), (g_oth, 1 - yh)):
        for s in range(4):
            from_z = lax.rem(z + 4 - s, 4)
            for col in range(8):
                place(ref[s, col], col + 8, from_z * 2 + from_yh)

    @pl.loop(0, 4)
    def _(i):
        acc[...] = jnp.zeros_like(acc)

        def add(copy, slot, tile):
            copy.wait()
            at = pl.ds(pl.multiple_of(tile * TILE, TILE), TILE)
            hi, lo = halves(tiles[i, slot])
            b_hi = f_hi[at, :]
            acc[...] += (
                jnp.dot(hi, b_hi, preferred_element_type=jnp.float32)
                + jnp.dot(lo, b_hi, preferred_element_type=jnp.float32)
                + jnp.dot(hi, f_lo[at, :], preferred_element_type=jnp.float32)
            )

        each(i, add)
        to_l = lax.div(i, 2)
        for b in range(2):
            step = lax.rem(lax.rem(i, 2) * 2 + b + 4 - x, 4)
            first = acc[b * 256 : b * 256 + 128, :]
            last = acc[b * 256 + 128 : b * 256 + 256, :]
            for s in range(4):

                @pl.when(step == s)
                def _():
                    outs[s][to_l] = first

            @pl.when(to_l == yl)
            def _():
                outs[4][step] = last

            @pl.when(to_l != yl)
            def _():
                outs[5][step] = last


def in_vmem(n):
    return [pl.BlockSpec(memory_space=pltpu.VMEM)] * n


def panel(info, own, oth, pieces):
    cols = pieces[0].shape[-1]
    out = [jax.ShapeDtypeStruct((2, 128, cols), jnp.float32)] * 4
    out += [jax.ShapeDtypeStruct((4, 128, cols), jnp.float32)] * 2
    return pl.pallas_call(
        panel_kernel,
        in_specs=[pl.BlockSpec(memory_space=pltpu.SMEM)]
        + [pl.BlockSpec(memory_space=pl.ANY)] * 2
        + in_vmem(6),
        out_specs=in_vmem(6),
        scratch_shapes=[
            pltpu.VMEM((2048, cols), jnp.bfloat16),
            pltpu.VMEM((2048, cols), jnp.bfloat16),
            pltpu.VMEM((TILE, cols), jnp.float32),
            pltpu.VMEM((4, 4, TILE, TILE), jnp.float32),
            pltpu.SemaphoreType.DMA((4, 4)),
        ],
        out_shape=out,
        compiler_params=pltpu.CompilerParams(vmem_limit_bytes=48 << 20),
        cost_estimate=pl.CostEstimate(
            flops=3 * 2 * 2048 * 2048 * cols,
            bytes_accessed=20 << 20,
            transcendentals=0,
        ),
    )(info, own, oth, *pieces)


def finish_kernel(info, *refs):
    parts, rows, (diag, keep, send, *lasts) = refs[:12], refs[12:18], refs[18:]
    yl = info[12]
    t_hi, t_lo = halves(jnp.concatenate([ref[...] for ref in rows], axis=1))
    for c in range(2):
        firsts, (mine, got) = parts[c * 6 : c * 6 + 4], parts[c * 6 + 4 : c * 6 + 6]
        here, away = (sum(ref[i] for ref in firsts) for i in (yl, 1 - yl))
        sums = [here, away] + [mine[s] + got[s] for s in range(4)]
        for ref, value in zip((keep, send, *lasts), sums):
            ref[c] = value
        p_hi, p_lo = halves(jnp.concatenate(sums, axis=0))
        cols = p_hi.shape[1]
        diag[:, c * cols : (c + 1) * cols] = (
            jnp.dot(t_hi, p_hi, preferred_element_type=jnp.float32)
            + jnp.dot(t_lo, p_hi, preferred_element_type=jnp.float32)
            + jnp.dot(t_hi, p_lo, preferred_element_type=jnp.float32)
        )


def finish(info, parts, rows):
    cols = parts[0].shape[-1]
    out = [jax.ShapeDtypeStruct((WIDTH, 2 * cols), jnp.float32)]
    out += [jax.ShapeDtypeStruct((2, 128, cols), jnp.float32)] * 6
    return pl.pallas_call(
        finish_kernel,
        in_specs=[pl.BlockSpec(memory_space=pltpu.SMEM)] + in_vmem(18),
        out_specs=in_vmem(7),
        out_shape=out,
        compiler_params=pltpu.CompilerParams(vmem_limit_bytes=24 << 20),
        cost_estimate=pl.CostEstimate(
            flops=3 * 4 * 768 * WIDTH * cols, bytes_accessed=9 << 20, transcendentals=0
        ),
    )(info, *parts, *rows)


def pick(v, i):
    return lax.dynamic_index_in_dim(v, i, 0, keepdims=False)


def per_device(ancestor, factor, diag_inverse, structure):
    z, yh, yl, x, core = (lax.axis_index(axis) for axis in AXES)
    row, group = z * 2 + yh, yl * 4 + x
    at_first = core == 0
    half = WIDTH // 2

    listed = pick(structure, core)
    four = jnp.arange(4, dtype=jnp.int32)
    flag = lambda tiles: jnp.any(listed[None, :] == tiles[:, None], axis=1)
    info = jnp.concatenate(
        [
            flag(row * 4 + four).astype(jnp.int32),
            flag(group * 4 + four).astype(jnp.int32),
            jnp.stack([core, z, yh, x, yl]).astype(jnp.int32),
        ]
    )

    oth = to_core(ancestor)

    turned = jnp.swapaxes(factor, 1, 2)
    f_keep = pick(turned, core)
    f_got = to_core(pick(turned, 1 - core))
    f_first = jnp.where(at_first, f_keep, f_got)
    f_last = jnp.where(at_first, f_got, f_keep)
    f_rows = [f_first, to_yl(f_first), f_last, *(to_x(f_last, s) for s in (3, 2, 1))]

    spread = lax.all_to_all(factor.reshape(2, 8, 16, WIDTH), ROW, 1, 0)
    spread = lax.all_to_all(spread.reshape(16, 16, WIDTH), COL, 0, 0)
    spread, info = lax.optimization_barrier((spread, info))
    gathered = []
    for c in range(2):
        low, high = (v[:, :, c * half : (c + 1) * half] for v in (spread[:8], spread[8:]))
        low_y, *high_z = lax.optimization_barrier(
            (to_y(low, 2), high, *(to_z(high, s) for s in (1, 2, 3)))
        )
        pair, quad = jnp.stack([low, low_y]), jnp.stack(high_z)
        pairs = [pair] + [to_z(pair, s) for s in (1, 2, 3)]
        gathered.append([*pairs, quad, to_y(quad, 2)])

    parts = []
    for c in range(2):
        first0, first1, first2, first3, last_keep, last_send = panel(
            info, ancestor, oth, gathered[c]
        )
        got = [to_x(first1, 1), to_x(first3, 3), to_x(first2, 2)]
        parts += [first0, *got, last_keep, to_yl(last_send)]

    diag, first, first_send, *last = finish(info, parts, f_rows)
    first = first + to_yl(first_send)
    last = last[0] + to_x(last[1], 1) + to_x(last[3], 3) + to_x(last[2], 2)
    mine = jnp.where(at_first, first, last)
    theirs = to_core(jnp.where(at_first, last, first))
    off = -jnp.where(at_first, jnp.stack([mine, theirs]), jnp.stack([theirs, mine]))
    off = jnp.concatenate([off[:, 0], off[:, 1]], axis=-1)

    diag = lax.all_to_all(diag.reshape(64, 8, WIDTH), CHIPS, 0, 0)
    own8 = ((row * 2 + yl) * 4 + x) * 8
    diag = jnp.sum(diag, axis=0)
    diag = diag + lax.dynamic_slice(diag_inverse, (core, own8, 0), (1, 8, WIDTH))[0]
    diag = lax.all_to_all(jnp.broadcast_to(diag, (64, 8, WIDTH)), CHIPS, 0, 0)
    diag = diag.reshape(WIDTH, WIDTH)
    diag_oth = to_core(diag)
    both = jnp.where(
        at_first, jnp.stack([diag, diag_oth]), jnp.stack([diag_oth, diag])
    )
    return off, both


def solution(mesh):
    mesh = Mesh(mesh.devices.reshape(4, 2, 2, 4, 2), AXES)
    in_specs = (P(ROW, COL), P(None, AXES, None), P(), P())
    out_specs = (P(None, AXES, None), P())

    return jax.shard_map(
        per_device, mesh=mesh, in_specs=in_specs, out_specs=out_specs, check_vma=False
    )
```

```python
import jax
import jax.numpy as jnp
from jax import lax
from jax.experimental import pallas as pl
from jax.experimental.pallas import tpu as pltpu
from jax.sharding import Mesh
from jax.sharding import PartitionSpec as P

TILE = 512
WIDTH = 512

ROW, COL = ("z", "yh"), ("yl", "x", "core")
AXES, CHIPS = ROW + COL, ROW + COL[:2]


def route(move):
    pairs = []
    for d in range(128):
        z, yh, yl, x, core = d // 32, d // 16 % 2, d // 8 % 2, d // 2 % 4, d % 2
        z, y, x, core = move(z, yh * 2 + yl, x, core)
        z, y, x = z % 4, y % 4, x % 4
        pairs.append((d, z * 32 + (y // 2) * 16 + (y % 2) * 8 + x * 2 + core))
    return pairs


def to_core(v):
    return lax.ppermute(v, AXES, route(lambda z, y, x, c: (z, y, x, 1 - c)))


def to_x(v, s):
    return lax.ppermute(v, AXES, route(lambda z, y, x, c: (z, y, x + s, c)))


def to_y(v, s):
    return lax.ppermute(v, AXES, route(lambda z, y, x, c: (z, y + s, x, c)))


def to_yl(v):
    return lax.ppermute(v, AXES, route(lambda z, y, x, c: (z, y ^ 1, x, c)))


def to_z(v, s):
    return lax.ppermute(v, AXES, route(lambda z, y, x, c: (z + s, y, x, c)))


def halves(a):
    hi = a.astype(jnp.bfloat16)
    return hi, (a - hi.astype(jnp.float32)).astype(jnp.bfloat16)


def panel_kernel(info, own, oth, f0, f1, f2, f3, g_own, g_oth, *rest):
    outs, (f_hi, f_lo, acc, tiles, sems) = rest[:6], rest[6:]
    core, z, yh, x, yl = info[8], info[9], info[10], info[11], info[12]

    def each(i, act):
        rows = pl.ds(pl.multiple_of(i * TILE, TILE), TILE)
        for s, (ref, side) in enumerate(((own, core), (oth, 1 - core))):
            for j in range(2):
                slot, tile = s * 2 + j, side * 2 + j
                copy = pltpu.make_async_copy(
                    ref.at[rows, pl.ds(j * TILE, TILE)], tiles.at[i, slot], sems.at[i, slot]
                )

                @pl.when((info[i] > 0) & (info[4 + tile] > 0))
                def _():
                    act(copy, slot, tile)

    @pl.loop(0, 4)
    def _(i):
        each(i, lambda copy, slot, tile: copy.start())

    def place(value, col, row):
        at = pl.ds(pl.multiple_of(col * 128 + row * 16, 16), 16)
        hi, lo = halves(value)
        f_hi[at, :] = hi
        f_lo[at, :] = lo

    for tile in range(4):

        @pl.when(info[4 + tile] > 0)
        def _():
            for col in range(tile * 4, tile * 4 + 4):
                for s in range(4):
                    from_z = lax.rem(z + 4 - s, 4)
                    for h, from_yh in enumerate((yh, 1 - yh)):
                        if col < 8:
                            piece = (f0, f1, f2, f3)[s][h, col]
                        else:
                            piece = (g_own, g_oth)[h][s, col - 8]
                        place(piece, col, from_z * 2 + from_yh)

    @pl.loop(0, 4)
    def _(i):
        acc[...] = jnp.zeros_like(acc)

        def add(copy, slot, tile):
            copy.wait()
            at = pl.ds(pl.multiple_of(tile * TILE, TILE), TILE)
            hi, lo = halves(tiles[i, slot])
            b_hi = f_hi[at, :]
            acc[...] += (
                jnp.dot(hi, b_hi, preferred_element_type=jnp.float32)
                + jnp.dot(lo, b_hi, preferred_element_type=jnp.float32)
                + jnp.dot(hi, f_lo[at, :], preferred_element_type=jnp.float32)
            )

        each(i, add)
        to_l = lax.div(i, 2)
        for b in range(2):
            step = lax.rem(lax.rem(i, 2) * 2 + b + 4 - x, 4)
            first = acc[b * 256 : b * 256 + 128, :]
            last = acc[b * 256 + 128 : b * 256 + 256, :]
            for s in range(4):

                @pl.when(step == s)
                def _():
                    outs[s][to_l] = first

            @pl.when(to_l == yl)
            def _():
                outs[4][step] = last

            @pl.when(to_l != yl)
            def _():
                outs[5][step] = last


def in_vmem(n):
    return [pl.BlockSpec(memory_space=pltpu.VMEM)] * n


def panel(info, own, oth, pieces):
    cols = pieces[0].shape[-1]
    out = [jax.ShapeDtypeStruct((2, 128, cols), jnp.float32)] * 4
    out += [jax.ShapeDtypeStruct((4, 128, cols), jnp.float32)] * 2
    return pl.pallas_call(
        panel_kernel,
        in_specs=[pl.BlockSpec(memory_space=pltpu.SMEM)]
        + [pl.BlockSpec(memory_space=pl.ANY)] * 2
        + in_vmem(6),
        out_specs=in_vmem(6),
        scratch_shapes=[
            pltpu.VMEM((2048, cols), jnp.bfloat16),
            pltpu.VMEM((2048, cols), jnp.bfloat16),
            pltpu.VMEM((TILE, cols), jnp.float32),
            pltpu.VMEM((4, 4, TILE, TILE), jnp.float32),
            pltpu.SemaphoreType.DMA((4, 4)),
        ],
        out_shape=out,
        compiler_params=pltpu.CompilerParams(vmem_limit_bytes=44 << 20),
        cost_estimate=pl.CostEstimate(
            flops=3 * 2 * 2048 * 2048 * cols,
            bytes_accessed=20 << 20,
            transcendentals=0,
        ),
    )(info, own, oth, *pieces)


def finish_kernel(info, *refs):
    parts, rows, (diag, keep, send, *lasts) = refs[:12], refs[12:18], refs[18:]
    yl = info[12]
    t_hi, t_lo = halves(jnp.concatenate([ref[...] for ref in rows], axis=1))
    for c in range(2):
        firsts, (mine, got) = parts[c * 6 : c * 6 + 4], parts[c * 6 + 4 : c * 6 + 6]
        here, away = (sum(ref[i] for ref in firsts) for i in (yl, 1 - yl))
        sums = [here, away] + [mine[s] + got[s] for s in range(4)]
        for ref, value in zip((keep, send, *lasts), sums):
            ref[c] = value
        p_hi, p_lo = halves(jnp.concatenate(sums, axis=0))
        cols = p_hi.shape[1]
        diag[:, c * cols : (c + 1) * cols] = (
            jnp.dot(t_hi, p_hi, preferred_element_type=jnp.float32)
            + jnp.dot(t_lo, p_hi, preferred_element_type=jnp.float32)
            + jnp.dot(t_hi, p_lo, preferred_element_type=jnp.float32)
        )


def finish(info, parts, rows):
    cols = parts[0].shape[-1]
    out = [jax.ShapeDtypeStruct((WIDTH, 2 * cols), jnp.float32)]
    out += [jax.ShapeDtypeStruct((2, 128, cols), jnp.float32)] * 6
    return pl.pallas_call(
        finish_kernel,
        in_specs=[pl.BlockSpec(memory_space=pltpu.SMEM)] + in_vmem(18),
        out_specs=in_vmem(7),
        out_shape=out,
        compiler_params=pltpu.CompilerParams(vmem_limit_bytes=24 << 20),
        cost_estimate=pl.CostEstimate(
            flops=3 * 4 * 768 * WIDTH * cols, bytes_accessed=9 << 20, transcendentals=0
        ),
    )(info, *parts, *rows)


def pick(v, i):
    return lax.dynamic_index_in_dim(v, i, 0, keepdims=False)


def per_device(ancestor, factor, diag_inverse, structure):
    z, yh, yl, x, core = (lax.axis_index(axis) for axis in AXES)
    row, group = z * 2 + yh, yl * 4 + x
    at_first = core == 0
    half = WIDTH // 2

    listed = pick(structure, core)
    four = jnp.arange(4, dtype=jnp.int32)
    flag = lambda tiles: jnp.any(listed[None, :] == tiles[:, None], axis=1)
    info = jnp.concatenate(
        [
            flag(row * 4 + four).astype(jnp.int32),
            flag(group * 4 + four).astype(jnp.int32),
            jnp.stack([core, z, yh, x, yl]).astype(jnp.int32),
        ]
    )

    oth = to_core(ancestor)

    turned = jnp.swapaxes(factor, 1, 2)
    f_keep = pick(turned, core)
    f_got = to_core(pick(turned, 1 - core))
    f_first = jnp.where(at_first, f_keep, f_got)
    f_last = jnp.where(at_first, f_got, f_keep)
    f_rows = [f_first, to_yl(f_first), f_last, *(to_x(f_last, s) for s in (3, 2, 1))]

    spread = lax.all_to_all(factor.reshape(2, 8, 16, WIDTH), ROW, 1, 0)
    spread = lax.all_to_all(spread.reshape(16, 16, WIDTH), COL, 0, 0)
    spread, info = lax.optimization_barrier((spread, info))
    gathered = []
    for c in range(2):
        low, high = (v[:, :, c * half : (c + 1) * half] for v in (spread[:8], spread[8:]))
        low_y, *high_z = lax.optimization_barrier(
            (to_y(low, 2), high, *(to_z(high, s) for s in (1, 2, 3)))
        )
        pair, quad = jnp.stack([low, low_y]), jnp.stack(high_z)
        pairs = [pair] + [to_z(pair, s) for s in (1, 2, 3)]
        gathered.append([*pairs, quad, to_y(quad, 2)])

    parts = []
    for c in range(2):
        first0, first1, first2, first3, last_keep, last_send = panel(
            info, ancestor, oth, gathered[c]
        )
        got = [to_x(first1, 1), to_x(first3, 3), to_x(first2, 2)]
        parts += [first0, *got, last_keep, to_yl(last_send)]

    diag, first, first_send, *last = finish(info, parts, f_rows)
    first = first + to_yl(first_send)
    last = last[0] + to_x(last[1], 1) + to_x(last[3], 3) + to_x(last[2], 2)
    mine = jnp.where(at_first, first, last)
    theirs = to_core(jnp.where(at_first, last, first))
    off = -jnp.where(at_first, jnp.stack([mine, theirs]), jnp.stack([theirs, mine]))
    off = jnp.concatenate([off[:, 0], off[:, 1]], axis=-1)

    diag = lax.all_to_all(diag.reshape(64, 8, WIDTH), CHIPS, 0, 0)
    own8 = ((row * 2 + yl) * 4 + x) * 8
    diag = jnp.sum(diag, axis=0)
    diag = diag + lax.dynamic_slice(diag_inverse, (core, own8, 0), (1, 8, WIDTH))[0]
    diag = lax.all_to_all(jnp.broadcast_to(diag, (64, 8, WIDTH)), CHIPS, 0, 0)
    diag = diag.reshape(WIDTH, WIDTH)
    diag_oth = to_core(diag)
    both = jnp.where(
        at_first, jnp.stack([diag, diag_oth]), jnp.stack([diag_oth, diag])
    )
    return off, both


def solution(mesh):
    mesh = Mesh(mesh.devices.reshape(4, 2, 2, 4, 2), AXES)
    in_specs = (P(ROW, COL), P(None, AXES, None), P(), P())
    out_specs = (P(None, AXES, None), P())

    return jax.shard_map(
        per_device, mesh=mesh, in_specs=in_specs, out_specs=out_specs, check_vma=False
    )
```
